32 devices in a mesh: groups: 2 (over y), row: 4 (over z), col: 2 (over x), sub: 2 (over core).
Axes of the slice: x: 2, y: 2, z: 4, core: 2. Of those that a mesh axis runs over, the one named last changes fastest.
Arguments:
- query_acts: bfloat16 [64, 128, 4096], P(('groups', 'col', 'sub'), None, 'row'), parts along dimension 0, may hold values from -6 to 6
- query_grads: bfloat16 [64, 128, 4096], P(('groups', 'col', 'sub'), None, 'row'), parts along dimension 0, may hold values from -0.5390625 to 0.5390625
- proj_in: bfloat16 [4096, 128], P('row'), may hold values from -0.09375 to 0.09375
- proj_out: bfloat16 [4096, 128], P('row'), may hold values from -0.09375 to 0.09375
- inverse_gram: float32 [16384, 16384], P('row', ('col', 'sub')), may hold values from -0.01 to 2.01, as said below
- store_slab: bfloat16 [2048, 16384], P(('groups', 'col'), ('row', 'sub')), parts along dimension 0, may hold values from -0.046875 to 0.046875
Outputs:
- scores: float32 [64, 1024], P('groups', 'col'), parts along dimension 0
The draws below stay inside these ranges and needn't reach their ends.
There are 2 independent parts, one for each index of `groups`. The reference program is written for one: setup_inputs(seed, part) draws one part's arguments, and reference() takes and returns one part's arrays. A program takes and returns all parts, laid end to end along the dimension named above; an argument that names none is the same for every part. Nothing has to cross between parts.
Inputs may be any that keep to these rules, and one draw needn't show every extreme that they name: inverse_gram is symmetric.
All inputs are finite; a program needn't handle non-finite values.
Results may differ from the reference program's by a relative error of at most 0.0029.
Values may be sent and summed in bfloat16 or wider, within the bound.
A program may use at most 128 MiB of HBM per device.

```python
import math
import jax
import jax.numpy as jnp
from jax import lax

D = 4096
K_IN = 128
K_OUT = 128
Q = 32
S = 128
F = 16384
E = 1024


def draw_inverse_gram(key, part):
    feature_count = K_IN * K_OUT
    first_key, second_key = jax.random.split(jax.random.fold_in(key, 11))
    noise = jax.random.uniform(first_key, (feature_count, feature_count), jnp.float32, -1.0, 1.0)
    symmetric = (noise + noise.T) * 0.005
    diagonal = jnp.exp(jax.random.uniform(second_key, (feature_count,), jnp.float32, math.log(0.5), math.log(2.0)))
    positions = jnp.arange(feature_count)
    return symmetric.at[positions, positions].add(diagonal)


def block_levels(own_key, extent, cuts, low, top_value):
    gain = 1.0
    for position, shards_of in cuts:
        steps = jax.random.uniform(jax.random.fold_in(jax.random.fold_in(own_key, 6), position), (shards_of,), jnp.float32, low / len(cuts), top_value / len(cuts))
        gain = gain * jnp.repeat(jnp.exp(steps), extent[position] // shards_of).reshape((-1,) + (1,) * (len(extent) - 1 - position))
    return gain


def bell_draw(key, dims, deviation, reach, pieces=(), kind=jnp.bfloat16):
    gain = block_levels(key, dims, pieces, -0.22, 0.18) if pieces else 1.0
    entries = jax.random.normal(key, dims, jnp.float32) * deviation * gain
    return jnp.minimum(jnp.maximum(entries, -reach), reach).astype(kind)


def setup_inputs(seed: int = 0, part: int = 0) -> dict:
    key_of = jax.random.split(jax.random.key(seed), 7)
    part_splits = jax.random.split(jax.random.fold_in(key_of[6], part), 7)
    return {
        "query_acts": bell_draw(part_splits[0], (Q, S, D), 1.0, 6.0, ((0, 4), (2, 4))),
        "query_grads": bell_draw(part_splits[1], (Q, S, D), 0.09, 0.5390625, ((0, 4), (2, 4))),
        "proj_in": bell_draw(key_of[2], (D, K_IN), D ** -0.5, 0.09375, ((0, 4),)),
        "proj_out": bell_draw(key_of[3], (D, K_OUT), D ** -0.5, 0.09375, ((0, 4),)),
        "inverse_gram": draw_inverse_gram(jax.random.fold_in(key_of[6], 71), part),
        "store_slab": bell_draw(part_splits[5], (E, F), F ** -0.5, 0.046875, ((0, 2), (1, 8))),
    }


def reference(query_acts, query_grads, proj_in, proj_out, inverse_gram, store_slab):
    act_proj = jnp.einsum("qtd,dk->qtk", query_acts.astype(jnp.float32), proj_in.astype(jnp.float32), precision=lax.Precision.HIGHEST)
    grad_proj = jnp.einsum("qtd,dk->qtk", query_grads.astype(jnp.float32), proj_out.astype(jnp.float32), precision=lax.Precision.HIGHEST)
    kron_feats = jnp.einsum("qta,qtb->qab", act_proj, grad_proj, precision=lax.Precision.HIGHEST)
    kron_feats = kron_feats.reshape(kron_feats.shape[0], -1)
    precond = jnp.dot(kron_feats, inverse_gram, precision=lax.Precision.HIGHEST)
    precond_b = precond.astype(jnp.bfloat16)
    return jnp.dot(precond_b, store_slab.T, preferred_element_type=jnp.float32)
```

```python
import functools

import jax
import jax.numpy as jnp
from jax import lax
from jax.experimental import pallas as pl
from jax.experimental.pallas import tpu as pltpu
from jax.sharding import PartitionSpec as P

F32, BF16 = jnp.float32, jnp.bfloat16
SLOTS = 9


def split(x):
    hi = x.astype(BF16)
    return hi, (x - hi.astype(F32)).astype(BF16)


def kernel(rows, cols, subs, acts_h, grads_h, pin_h, pout_h, gram_h, store_h, out,
           acts, grads, pin, pout, gram, store, part, recv, feats, fbuf, ft, pt, pre, sub_in, col_in,
           own, own_s, half_in, half_all, half_out,
           in_sem, gram_sem, rs_send, rs_recv, fx_send, fx_recv, fx_local, fz_send, fz_recv,
           ps_sem, pc_send, pc_recv, ss_sem, sz_send, sz_recv, sl_sem, sf_sem):
    g, r, c, s = (lax.axis_index(n) for n in ("groups", "row", "col", "sub"))
    queries = acts.shape[0]
    half = queries // 2
    planes = cols * subs
    me = c * subs + s
    aw = fbuf.shape[2]
    mb, kb = gram.shape[1], gram.shape[2]
    grows, gcols = gram_h.shape
    nk, ni = gcols // kb, grows // mb
    blocks = nk * ni

    def dev(row, col, sub):
        return {"groups": g, "row": row, "col": col, "sub": sub}

    def remote(src, dst, send, rcv, row, col, sub):
        return pltpu.make_async_remote_copy(
            src_ref=src, dst_ref=dst, send_sem=send, recv_sem=rcv,
            device_id=dev(row, col, sub), device_id_type=pl.DeviceIdType.MESH)

    loads = [pltpu.make_async_copy(a, b, in_sem.at[i]) for i, (a, b) in enumerate(
        ((pin_h, pin), (pout_h, pout), (acts_h, acts), (grads_h, grads), (store_h, store)))]
    for l in loads[:4]:
        l.start()

    def gram_copy(b):
        k, i = b // ni, b % ni
        slot = lax.rem(b, SLOTS)
        return pltpu.make_async_copy(
            gram_h.at[pl.ds(pl.multiple_of(i * mb, mb), mb), pl.ds(pl.multiple_of(k * kb, kb), kb)],
            gram.at[slot], gram_sem.at[slot])

    for b in range(min(SLOTS, blocks)):
        gram_copy(b).start()
    loads[4].start()

    barrier = pltpu.get_barrier_semaphore()
    count = 0
    for d in range(1, rows):
        pl.semaphore_signal(barrier, inc=1, device_id=dev(lax.rem(r + d, rows), c, s), device_id_type=pl.DeviceIdType.MESH)
        count += 1
    for d in range(1, planes):
        o = lax.rem(me + d, planes)
        pl.semaphore_signal(barrier, inc=1, device_id=dev(r, o // subs, lax.rem(o, subs)), device_id_type=pl.DeviceIdType.MESH)
        count += 1

    def project(q):
        part[q, 0] = jnp.dot(acts[q], pin[...], preferred_element_type=F32)
        part[q, 1] = jnp.dot(grads[q], pout[...], preferred_element_type=F32)

    for l in loads[:4]:
        l.wait()
    for q in range(queries):
        project(q)
    pl.semaphore_wait(barrier, count)

    starts = (r == 0, r == rows - 1)
    ends = (r == rows - 1, r == 0)
    ahead = (jnp.minimum(r + 1, rows - 1), jnp.maximum(r - 1, 0))
    behind = (jnp.maximum(r - 1, 0), jnp.minimum(r + 1, rows - 1))

    def rs_copy(h, q, w):
        return remote(part.at[q, w], recv.at[q, w], rs_send.at[q, w], rs_recv.at[q, w], ahead[h], c, s)

    def fx_copy(q, d):
        o = lax.rem(me + d, planes)
        return remote(feats.at[lax.rem(q, half), pl.ds(pl.multiple_of(o * aw, aw), aw)], fbuf.at[me, q],
                      fx_send.at[lax.rem(q, half), d], fx_recv.at[lax.rem(q, half), d], r, o // subs, lax.rem(o, subs))

    def fx_own(q):
        return pltpu.make_async_copy(feats.at[lax.rem(q, half), pl.ds(pl.multiple_of(me * aw, aw), aw)],
                                     fbuf.at[me, q], fx_local.at[lax.rem(q, half)])

    def fz_copy(h, q):
        return remote(fbuf.at[:, q], fbuf.at[:, q], fz_send.at[q], fz_recv.at[q], behind[h], c, s)

    def send_row(h, q):
        for d in range(1, planes):
            fx_copy(q, d).wait()
        fx_own(q).wait()
        fz_copy(h, q).start()

    for k in range(half):
        for w in range(2):
            for h in range(2):
                q = h * half + k

                @pl.when(jnp.logical_not(starts[h]))
                def _():
                    rs_copy(h, q, w).wait_recv()
                    part[q, w] = part[q, w] + recv[q, w]

                @pl.when(jnp.logical_not(ends[h]))
                def _():
                    rs_copy(h, q, w).start()
        for h in range(2):
            q = h * half + k

            @pl.when(ends[h])
            def _():
                feats[k] = jnp.dot(part[q, 0].T, part[q, 1], precision=lax.Precision.HIGHEST,
                                   preferred_element_type=F32)
                for d in range(1, planes):
                    fx_copy(q, d).start()
                fx_own(q).start()
                if k:
                    send_row(h, q - 1)
    for h in range(2):
        @pl.when(ends[h])
        def _():
            send_row(h, h * half + half - 1)

    for k in range(half):
        for h in range(2):
            q = h * half + k

            @pl.when(jnp.logical_not(ends[h]))
            def _():
                fz_copy(h, q).wait_recv()

            @pl.when(jnp.logical_not(jnp.logical_or(starts[h], ends[h])))
            def _():
                fz_copy(h, q).start()
    for k in range(half):
        for h in range(2):
            q = h * half + k

            @pl.when(jnp.logical_not(starts[h]))
            def _():
                fz_copy(h, q).wait_send()

            @pl.when(jnp.logical_not(ends[h]))
            def _():
                for w in range(2):
                    rs_copy(h, q, w).wait_send()

    nq = planes * queries
    width = ft.shape[1]
    for a in range(aw):
        x = fbuf[:, :, a, :].reshape(nq, fbuf.shape[3])
        hi, lo = split(x)
        hi, lo = hi.astype(F32), lo.astype(F32)
        rest = [jnp.zeros((width - 2 * nq, x.shape[1]), F32)] if width > 2 * nq else []
        y = jnp.concatenate([hi, lo] + rest, axis=0)
        ft[a * x.shape[1]:(a + 1) * x.shape[1], :] = y.T.astype(BF16)

    step = min(256, mb)

    def block(b, _):
        k, i = b // ni, b % ni
        slot = lax.rem(b, SLOTS)
        gram_copy(b).wait()
        w = ft[pl.ds(pl.multiple_of(k * kb, kb), kb), :]

        def inner(m, _):
            rows_at = pl.multiple_of(m * step, step)
            hi, lo = split(gram[slot, pl.ds(rows_at, step), :])
            acc = jnp.dot(hi, w, preferred_element_type=F32) + jnp.dot(lo, w, preferred_element_type=F32)
            at = pl.ds(pl.multiple_of(i * mb + m * step, step), step)

            @pl.when(k == 0)
            def _():
                pt[at, :] = acc

            @pl.when(k > 0)
            def _():
                pt[at, :] = pt[at, :] + acc
            return 0

        lax.fori_loop(0, mb // step, inner, 0)

        @pl.when(b + SLOTS < blocks)
        def _():
            gram_copy(b + SLOTS).start()
        return 0

    lax.fori_loop(0, blocks, block, 0)

    tile = 128
    for j in range(grows // tile):
        t = pt[j * tile:(j + 1) * tile, :].T
        per = pre.shape[2] // tile
        pre[j // per, :, (j % per) * tile:(j % per + 1) * tile] = t[:nq] + t[nq:2 * nq]
    other = lax.rem(s + 1, subs)
    x_sub = remote(pre.at[other], sub_in, ps_sem.at[0], ps_sem.at[1], r, c, other)
    x_sub.start()
    x_sub.wait()
    pre[s] = pre[s] + sub_in[...]
    x_cols = [remote(pre.at[s], col_in.at[c], pc_send.at[d], pc_recv.at[d], r, lax.rem(c + d, cols), s)
              for d in range(1, cols)]
    for x in x_cols:
        x.start()
    col_in[c] = pre[s]
    for x in x_cols:
        x.wait()
    total = col_in[0]
    for o in range(1, cols):
        total = total + col_in[o]
    loads[4].wait()
    score = lax.dot_general(total.astype(BF16), store[...], (((1,), (1,)), ((), ())), preferred_element_type=F32)

    hq = nq // subs
    for o in range(subs):
        own[o] = score[o * hq:(o + 1) * hq]
    x_half = remote(own.at[other], half_in, ss_sem.at[0], ss_sem.at[1], r, c, other)
    x_half.start()
    x_half.wait()
    own_s[...] = own[s] + half_in[...]
    x_rows = [remote(own_s, half_all.at[r], sz_send.at[d], sz_recv.at[d], lax.rem(r + d, rows), c, s)
              for d in range(1, rows)]
    for x in x_rows:
        x.start()
    half_all[r] = own_s[...]
    for x in x_rows:
        x.wait()
    total = half_all[0]
    for o in range(1, rows):
        total = total + half_all[o]
    half_out[s] = total
    x_out = remote(half_out.at[s], half_out.at[s], sf_sem.at[0], sf_sem.at[1], r, c, other)
    x_out.start()
    x_out.wait()
    for o in range(subs):
        out[o * hq:(o + 1) * hq, :] = half_out[o]


def body(sizes, query_acts, query_grads, proj_in, proj_out, inverse_gram, store_slab):
    rows, cols, subs = sizes
    queries, tokens, depth = query_acts.shape
    kin, kout = proj_in.shape[1], proj_out.shape[1]
    planes = cols * subs
    nq = planes * queries
    aw = kin // planes
    grows, gcols = inverse_gram.shape
    mb, kb = min(512, grows), min(2048, gcols)
    examples, width = store_slab.shape
    half = queries // 2
    hq = nq // subs
    dma = pltpu.SemaphoreType.DMA
    lanes = -(-2 * nq // 128) * 128
    scratch = [
        pltpu.VMEM(query_acts.shape, BF16), pltpu.VMEM(query_grads.shape, BF16),
        pltpu.VMEM(proj_in.shape, BF16), pltpu.VMEM(proj_out.shape, BF16),
        pltpu.VMEM((SLOTS, mb, kb), F32), pltpu.VMEM(store_slab.shape, BF16),
        pltpu.VMEM((queries, 2, tokens, kin), F32), pltpu.VMEM((queries, 2, tokens, kin), F32),
        pltpu.VMEM((half, kin, kout), F32), pltpu.VMEM((planes, queries, aw, kout), F32),
        pltpu.VMEM((gcols, lanes), BF16), pltpu.VMEM((grows, lanes), F32),
        pltpu.VMEM((subs, nq, width), F32), pltpu.VMEM((nq, width), F32), pltpu.VMEM((cols, nq, width), F32),
        pltpu.VMEM((subs, hq, examples), F32), pltpu.VMEM((hq, examples), F32), pltpu.VMEM((hq, examples), F32),
        pltpu.VMEM((rows, hq, examples), F32), pltpu.VMEM((subs, hq, examples), F32),
        dma((5,)), dma((SLOTS,)), dma((queries, 2)), dma((queries, 2)),
        dma((half, planes)), dma((half, planes)), dma((half,)), dma((queries,)), dma((queries,)),
        dma((2,)), dma((cols,)), dma((cols,)), dma((2,)), dma((rows,)), dma((rows,)), dma((1,)), dma((2,)),
    ]
    return pl.pallas_call(
        functools.partial(kernel, rows, cols, subs),
        out_shape=jax.ShapeDtypeStruct((nq, examples), F32),
        in_specs=[pl.BlockSpec(memory_space=pltpu.HBM)] * 6,
        out_specs=pl.BlockSpec(memory_space=pltpu.VMEM),
        scratch_shapes=scratch,
        compiler_params=pltpu.CompilerParams(
            collective_id=0, has_side_effects=True, vmem_limit_bytes=67043328),
        name="influence",
    )(query_acts, query_grads, proj_in, proj_out, inverse_gram, store_slab)


def solution(mesh):
    sizes = (mesh.shape["row"], mesh.shape["col"], mesh.shape["sub"])
    return jax.shard_map(
        functools.partial(body, sizes),
        mesh=mesh,
        in_specs=(
            P(("groups", "col", "sub"), None, "row"),
            P(("groups", "col", "sub"), None, "row"),
            P("row", None),
            P("row", None),
            P("row", ("col", "sub")),
            P(("groups", "col"), ("row", "sub")),
        ),
        out_specs=P("groups", "col"),
        check_vma=False,
    )
```

```python
import functools

import jax
import jax.numpy as jnp
from jax import lax
from jax.experimental import pallas as pl
from jax.experimental.pallas import tpu as pltpu
from jax.sharding import PartitionSpec as P

F32, BF16 = jnp.float32, jnp.bfloat16
SLOTS = 9


def split(x):
    hi = x.astype(BF16)
    return hi, (x - hi.astype(F32)).astype(BF16)


def kernel(rows, cols, subs, acts_h, grads_h, pin_h, pout_h, gram_h, store_h, out,
           acts, grads, pin, pout, gram, store, part, recv, feats, fbuf, ft, pt, pre, sub_in, col_in,
           own, own_s, half_in, half_all, half_out,
           in_sem, gram_sem, rs_send, rs_recv, fx_send, fx_recv, fx_local, fz_send, fz_recv,
           ps_sem, pc_send, pc_recv, ss_sem, sz_send, sz_recv, sl_sem, sf_sem):
    g, r, c, s = (lax.axis_index(n) for n in ("groups", "row", "col", "sub"))
    queries = acts.shape[0]
    half = queries // 2
    planes = cols * subs
    me = c * subs + s
    aw = fbuf.shape[2]
    mb, kb = gram.shape[1], gram.shape[2]
    grows, gcols = gram_h.shape
    nk, ni = gcols // kb, grows // mb
    blocks = nk * ni

    def dev(row, col, sub):
        return {"groups": g, "row": row, "col": col, "sub": sub}

    def remote(src, dst, send, rcv, row, col, sub):
        return pltpu.make_async_remote_copy(
            src_ref=src, dst_ref=dst, send_sem=send, recv_sem=rcv,
            device_id=dev(row, col, sub), device_id_type=pl.DeviceIdType.MESH)

    loads = [pltpu.make_async_copy(a, b, in_sem.at[i]) for i, (a, b) in enumerate(
        ((pin_h, pin), (pout_h, pout), (acts_h, acts), (grads_h, grads), (store_h, store)))]
    for l in loads[:4]:
        l.start()

    def gram_copy(b):
        k, i = b // ni, b % ni
        slot = lax.rem(b, SLOTS)
        return pltpu.make_async_copy(
            gram_h.at[pl.ds(pl.multiple_of(i * mb, mb), mb), pl.ds(pl.multiple_of(k * kb, kb), kb)],
            gram.at[slot], gram_sem.at[slot])

    for b in range(min(SLOTS, blocks)):
        gram_copy(b).start()
    loads[4].start()

    barrier = pltpu.get_barrier_semaphore()
    count = 0
    for d in range(1, rows):
        pl.semaphore_signal(barrier, inc=1, device_id=dev(lax.rem(r + d, rows), c, s), device_id_type=pl.DeviceIdType.MESH)
        count += 1
    for d in range(1, planes):
        o = lax.rem(me + d, planes)
        pl.semaphore_signal(barrier, inc=1, device_id=dev(r, o // subs, lax.rem(o, subs)), device_id_type=pl.DeviceIdType.MESH)
        count += 1

    def project(q):
        part[q, 0] = jnp.dot(acts[q], pin[...], preferred_element_type=F32)
        part[q, 1] = jnp.dot(grads[q], pout[...], preferred_element_type=F32)

    for l in loads[:4]:
        l.wait()
    for q in range(queries):
        project(q)
    pl.semaphore_wait(barrier, count)

    starts = (r == 0, r == rows - 1)
    ends = (r == rows - 1, r == 0)
    ahead = (jnp.minimum(r + 1, rows - 1), jnp.maximum(r - 1, 0))
    behind = (jnp.maximum(r - 1, 0), jnp.minimum(r + 1, rows - 1))

    def rs_copy(h, q, w):
        return remote(part.at[q, w], recv.at[q, w], rs_send.at[q, w], rs_recv.at[q, w], ahead[h], c, s)

    def fx_copy(q, d):
        o = lax.rem(me + d, planes)
        return remote(feats.at[lax.rem(q, half), pl.ds(pl.multiple_of(o * aw, aw), aw)], fbuf.at[me, q],
                      fx_send.at[lax.rem(q, half), d], fx_recv.at[lax.rem(q, half), d], r, o // subs, lax.rem(o, subs))

    def fx_own(q):
        return pltpu.make_async_copy(feats.at[lax.rem(q, half), pl.ds(pl.multiple_of(me * aw, aw), aw)],
                                     fbuf.at[me, q], fx_local.at[lax.rem(q, half)])

    def fz_copy(h, q):
        return remote(fbuf.at[:, q], fbuf.at[:, q], fz_send.at[q], fz_recv.at[q], behind[h], c, s)

    def send_row(h, q):
        for d in range(1, planes):
            fx_copy(q, d).wait()
        fx_own(q).wait()
        fz_copy(h, q).start()

    def sums(t, _):
        for h in range(2):
            j = t - (r if h == 0 else rows - 1 - r)
            k, w = j // 2, lax.rem(j, 2)
            q = h * half + k
            live = jnp.logical_and(j >= 0, j < 2 * half)

            @pl.when(jnp.logical_and(live, jnp.logical_not(starts[h])))
            def _():
                rs_copy(h, q, w).wait_recv()
                part[q, w] = part[q, w] + recv[q, w]

            @pl.when(jnp.logical_and(live, jnp.logical_not(ends[h])))
            def _():
                rs_copy(h, q, w).start()

            @pl.when(jnp.logical_and(jnp.logical_and(live, ends[h]), w == 1))
            def _():
                feats[k] = jnp.dot(part[q, 0].T, part[q, 1], precision=lax.Precision.HIGHEST,
                                   preferred_element_type=F32)
                for d in range(1, planes):
                    fx_copy(q, d).start()
                fx_own(q).start()

                @pl.when(k > 0)
                def _():
                    send_row(h, q - 1)
        return 0

    lax.fori_loop(0, 2 * half + rows - 1, sums, 0)
    for h in range(2):
        @pl.when(ends[h])
        def _():
            send_row(h, h * half + half - 1)

    def back(t, _):
        for h in range(2):
            k = t - (rows - 1 - r if h == 0 else r)
            q = h * half + k
            live = jnp.logical_and(k >= 0, k < half)

            @pl.when(jnp.logical_and(live, jnp.logical_not(ends[h])))
            def _():
                fz_copy(h, q).wait_recv()

            @pl.when(jnp.logical_and(live, jnp.logical_not(jnp.logical_or(starts[h], ends[h]))))
            def _():
                fz_copy(h, q).start()
        return 0

    lax.fori_loop(0, half + rows - 1, back, 0)
    for k in range(half):
        for h in range(2):
            q = h * half + k

            @pl.when(jnp.logical_not(starts[h]))
            def _():
                fz_copy(h, q).wait_send()

            @pl.when(jnp.logical_not(ends[h]))
            def _():
                for w in range(2):
                    rs_copy(h, q, w).wait_send()

    nq = planes * queries
    width = ft.shape[1]
    for a in range(aw):
        x = fbuf[:, :, a, :].reshape(nq, fbuf.shape[3])
        hi, lo = split(x)
        hi, lo = hi.astype(F32), lo.astype(F32)
        rest = [jnp.zeros((width - 2 * nq, x.shape[1]), F32)] if width > 2 * nq else []
        y = jnp.concatenate([hi, lo] + rest, axis=0)
        ft[a * x.shape[1]:(a + 1) * x.shape[1], :] = y.T.astype(BF16)

    step = min(256, mb)

    def block(b, _):
        k, i = b // ni, b % ni
        slot = lax.rem(b, SLOTS)
        gram_copy(b).wait()
        w = ft[pl.ds(pl.multiple_of(k * kb, kb), kb), :]

        def inner(m, _):
            rows_at = pl.multiple_of(m * step, step)
            hi, lo = split(gram[slot, pl.ds(rows_at, step), :])
            acc = jnp.dot(hi, w, preferred_element_type=F32) + jnp.dot(lo, w, preferred_element_type=F32)
            at = pl.ds(pl.multiple_of(i * mb + m * step, step), step)

            @pl.when(k == 0)
            def _():
                pt[at, :] = acc

            @pl.when(k > 0)
            def _():
                pt[at, :] = pt[at, :] + acc
            return 0

        lax.fori_loop(0, mb // step, inner, 0)

        @pl.when(b + SLOTS < blocks)
        def _():
            gram_copy(b + SLOTS).start()
        return 0

    lax.fori_loop(0, blocks, block, 0)

    tile = 128
    for j in range(grows // tile):
        t = pt[j * tile:(j + 1) * tile, :].T
        per = pre.shape[2] // tile
        pre[j // per, :, (j % per) * tile:(j % per + 1) * tile] = t[:nq] + t[nq:2 * nq]
    other = lax.rem(s + 1, subs)
    x_sub = remote(pre.at[other], sub_in, ps_sem.at[0], ps_sem.at[1], r, c, other)
    x_sub.start()
    x_sub.wait()
    pre[s] = pre[s] + sub_in[...]
    x_cols = [remote(pre.at[s], col_in.at[c], pc_send.at[d], pc_recv.at[d], r, lax.rem(c + d, cols), s)
              for d in range(1, cols)]
    for x in x_cols:
        x.start()
    col_in[c] = pre[s]
    for x in x_cols:
        x.wait()
    total = col_in[0]
    for o in range(1, cols):
        total = total + col_in[o]
    loads[4].wait()
    score = lax.dot_general(total.astype(BF16), store[...], (((1,), (1,)), ((), ())), preferred_element_type=F32)

    hq = nq // subs
    for o in range(subs):
        own[o] = score[o * hq:(o + 1) * hq]
    x_half = remote(own.at[other], half_in, ss_sem.at[0], ss_sem.at[1], r, c, other)
    x_half.start()
    x_half.wait()
    own_s[...] = own[s] + half_in[...]
    x_rows = [remote(own_s, half_all.at[r], sz_send.at[d], sz_recv.at[d], lax.rem(r + d, rows), c, s)
              for d in range(1, rows)]
    for x in x_rows:
        x.start()
    half_all[r] = own_s[...]
    for x in x_rows:
        x.wait()
    total = half_all[0]
    for o in range(1, rows):
        total = total + half_all[o]
    half_out[s] = total
    x_out = remote(half_out.at[s], half_out.at[s], sf_sem.at[0], sf_sem.at[1], r, c, other)
    x_out.start()
    x_out.wait()
    for o in range(subs):
        out[o * hq:(o + 1) * hq, :] = half_out[o]


def body(sizes, query_acts, query_grads, proj_in, proj_out, inverse_gram, store_slab):
    rows, cols, subs = sizes
    queries, tokens, depth = query_acts.shape
    kin, kout = proj_in.shape[1], proj_out.shape[1]
    planes = cols * subs
    nq = planes * queries
    aw = kin // planes
    grows, gcols = inverse_gram.shape
    mb, kb = min(512, grows), min(2048, gcols)
    examples, width = store_slab.shape
    half = queries // 2
    hq = nq // subs
    dma = pltpu.SemaphoreType.DMA
    lanes = -(-2 * nq // 128) * 128
    scratch = [
        pltpu.VMEM(query_acts.shape, BF16), pltpu.VMEM(query_grads.shape, BF16),
        pltpu.VMEM(proj_in.shape, BF16), pltpu.VMEM(proj_out.shape, BF16),
        pltpu.VMEM((SLOTS, mb, kb), F32), pltpu.VMEM(store_slab.shape, BF16),
        pltpu.VMEM((queries, 2, tokens, kin), F32), pltpu.VMEM((queries, 2, tokens, kin), F32),
        pltpu.VMEM((half, kin, kout), F32), pltpu.VMEM((planes, queries, aw, kout), F32),
        pltpu.VMEM((gcols, lanes), BF16), pltpu.VMEM((grows, lanes), F32),
        pltpu.VMEM((subs, nq, width), F32), pltpu.VMEM((nq, width), F32), pltpu.VMEM((cols, nq, width), F32),
        pltpu.VMEM((subs, hq, examples), F32), pltpu.VMEM((hq, examples), F32), pltpu.VMEM((hq, examples), F32),
        pltpu.VMEM((rows, hq, examples), F32), pltpu.VMEM((subs, hq, examples), F32),
        dma((5,)), dma((SLOTS,)), dma((queries, 2)), dma((queries, 2)),
        dma((half, planes)), dma((half, planes)), dma((half,)), dma((queries,)), dma((queries,)),
        dma((2,)), dma((cols,)), dma((cols,)), dma((2,)), dma((rows,)), dma((rows,)), dma((1,)), dma((2,)),
    ]
    return pl.pallas_call(
        functools.partial(kernel, rows, cols, subs),
        out_shape=jax.ShapeDtypeStruct((nq, examples), F32),
        in_specs=[pl.BlockSpec(memory_space=pltpu.HBM)] * 6,
        out_specs=pl.BlockSpec(memory_space=pltpu.VMEM),
        scratch_shapes=scratch,
        compiler_params=pltpu.CompilerParams(
            collective_id=0, has_side_effects=True, vmem_limit_bytes=67043328),
        name="influence",
    )(query_acts, query_grads, proj_in, proj_out, inverse_gram, store_slab)


def solution(mesh):
    sizes = (mesh.shape["row"], mesh.shape["col"], mesh.shape["sub"])
    return jax.shard_map(
        functools.partial(body, sizes),
        mesh=mesh,
        in_specs=(
            P(("groups", "col", "sub"), None, "row"),
            P(("groups", "col", "sub"), None, "row"),
            P("row", None),
            P("row", None),
            P("row", ("col", "sub")),
            P(("groups", "col"), ("row", "sub")),
        ),
        out_specs=P("groups", "col"),
        check_vma=False,
    )
```

```python
import functools

import jax
import jax.numpy as jnp
from jax import lax
from jax.experimental import pallas as pl
from jax.experimental.pallas import tpu as pltpu
from jax.sharding import PartitionSpec as P

F32, BF16 = jnp.float32, jnp.bfloat16
SLOTS = 9
LAG = 2


def split(x):
    hi = x.astype(BF16)
    return hi, (x - hi.astype(F32)).astype(BF16)


def kernel(rows, cols, subs, acts_h, grads_h, pin_h, pout_h, gram_h, store_h, out,
           acts, grads, pin, pout, gram, store, part, recv, feats, fbuf, ft, pt, pre, sub_in, col_in,
           own, own_s, half_in, half_all, half_out,
           in_sem, gram_sem, rs_send, rs_recv, fx_send, fx_recv, fx_local, fz_send, fz_recv,
           ps_sem, pc_send, pc_recv, ss_sem, sz_send, sz_recv, sl_sem, sf_sem):
    g, r, c, s = (lax.axis_index(n) for n in ("groups", "row", "col", "sub"))
    queries = acts.shape[0]
    half = queries // 2
    planes = cols * subs
    me = c * subs + s
    aw = fbuf.shape[2]
    mb, kb = gram.shape[1], gram.shape[2]
    grows, gcols = gram_h.shape
    nk, ni = gcols // kb, grows // mb
    blocks = nk * ni

    def dev(row, col, sub):
        return {"groups": g, "row": row, "col": col, "sub": sub}

    def remote(src, dst, send, rcv, row, col, sub):
        return pltpu.make_async_remote_copy(
            src_ref=src, dst_ref=dst, send_sem=send, recv_sem=rcv,
            device_id=dev(row, col, sub), device_id_type=pl.DeviceIdType.MESH)

    loads = [pltpu.make_async_copy(a, b, in_sem.at[i]) for i, (a, b) in enumerate(
        ((pin_h, pin), (pout_h, pout), (acts_h, acts), (grads_h, grads), (store_h, store)))]
    for l in loads[:4]:
        l.start()

    def gram_copy(b):
        k, i = b // ni, b % ni
        slot = lax.rem(b, SLOTS)
        return pltpu.make_async_copy(
            gram_h.at[pl.ds(pl.multiple_of(i * mb, mb), mb), pl.ds(pl.multiple_of(k * kb, kb), kb)],
            gram.at[slot], gram_sem.at[slot])

    for b in range(min(SLOTS, blocks)):
        gram_copy(b).start()
    loads[4].start()

    barrier = pltpu.get_barrier_semaphore()
    count = 0
    for d in range(1, rows):
        pl.semaphore_signal(barrier, inc=1, device_id=dev(lax.rem(r + d, rows), c, s), device_id_type=pl.DeviceIdType.MESH)
        count += 1
    for d in range(1, planes):
        o = lax.rem(me + d, planes)
        pl.semaphore_signal(barrier, inc=1, device_id=dev(r, o // subs, lax.rem(o, subs)), device_id_type=pl.DeviceIdType.MESH)
        count += 1

    def project(q):
        part[q, 0] = jnp.dot(acts[q], pin[...], preferred_element_type=F32)
        part[q, 1] = jnp.dot(grads[q], pout[...], preferred_element_type=F32)

    for l in loads[:4]:
        l.wait()
    for q in range(queries):
        project(q)
    pl.semaphore_wait(barrier, count)

    starts = (r == 0, r == rows - 1)
    ends = (r == rows - 1, r == 0)
    ahead = (jnp.minimum(r + 1, rows - 1), jnp.maximum(r - 1, 0))
    behind = (jnp.maximum(r - 1, 0), jnp.minimum(r + 1, rows - 1))

    def rs_copy(h, q, w):
        return remote(part.at[q, w], recv.at[q, w], rs_send.at[q, w], rs_recv.at[q, w], ahead[h], c, s)

    def fx_copy(q, d):
        o = lax.rem(me + d, planes)
        return remote(feats.at[lax.rem(q, half), pl.ds(pl.multiple_of(o * aw, aw), aw)], fbuf.at[me, q],
                      fx_send.at[lax.rem(q, half), d], fx_recv.at[lax.rem(q, half), d], r, o // subs, lax.rem(o, subs))

    def fx_own(q):
        return pltpu.make_async_copy(feats.at[lax.rem(q, half), pl.ds(pl.multiple_of(me * aw, aw), aw)],
                                     fbuf.at[me, q], fx_local.at[lax.rem(q, half)])

    def fz_copy(h, q):
        return remote(fbuf.at[:, q], fbuf.at[:, q], fz_send.at[q], fz_recv.at[q], behind[h], c, s)

    def send_row(h, q):
        for d in range(1, planes):
            fx_copy(q, d).wait()
        fx_own(q).wait()
        fz_copy(h, q).start()

    def sums(t, _):
        for h in range(2):
            j = t - LAG * (r if h == 0 else rows - 1 - r)
            k, w = j // 2, lax.rem(j, 2)
            q = h * half + k
            live = jnp.logical_and(j >= 0, j < 2 * half)

            @pl.when(jnp.logical_and(live, jnp.logical_not(starts[h])))
            def _():
                rs_copy(h, q, w).wait_recv()
                part[q, w] = part[q, w] + recv[q, w]

            @pl.when(jnp.logical_and(live, jnp.logical_not(ends[h])))
            def _():
                rs_copy(h, q, w).start()

            @pl.when(jnp.logical_and(jnp.logical_and(live, ends[h]), w == 1))
            def _():
                feats[k] = jnp.dot(part[q, 0].T, part[q, 1], precision=lax.Precision.HIGHEST,
                                   preferred_element_type=F32)
                for d in range(1, planes):
                    fx_copy(q, d).start()
                fx_own(q).start()

                @pl.when(k > 0)
                def _():
                    send_row(h, q - 1)
        return 0

    lax.fori_loop(0, 2 * half + LAG * (rows - 1), sums, 0)
    for h in range(2):
        @pl.when(ends[h])
        def _():
            send_row(h, h * half + half - 1)

    def back(t, _):
        for h in range(2):
            k = t - LAG * (rows - 1 - r if h == 0 else r)
            q = h * half + k
            live = jnp.logical_and(k >= 0, k < half)

            @pl.when(jnp.logical_and(live, jnp.logical_not(ends[h])))
            def _():
                fz_copy(h, q).wait_recv()

            @pl.when(jnp.logical_and(live, jnp.logical_not(jnp.logical_or(starts[h], ends[h]))))
            def _():
                fz_copy(h, q).start()
        return 0

    lax.fori_loop(0, half + LAG * (rows - 1), back, 0)
    for k in range(half):
        for h in range(2):
            q = h * half + k

            @pl.when(jnp.logical_not(starts[h]))
            def _():
                fz_copy(h, q).wait_send()

            @pl.when(jnp.logical_not(ends[h]))
            def _():
                for w in range(2):
                    rs_copy(h, q, w).wait_send()

    nq = planes * queries
    width = ft.shape[1]
    for a in range(aw):
        x = fbuf[:, :, a, :].reshape(nq, fbuf.shape[3])
        hi, lo = split(x)
        hi, lo = hi.astype(F32), lo.astype(F32)
        rest = [jnp.zeros((width - 2 * nq, x.shape[1]), F32)] if width > 2 * nq else []
        y = jnp.concatenate([hi, lo] + rest, axis=0)
        ft[a * x.shape[1]:(a + 1) * x.shape[1], :] = y.T.astype(BF16)

    step = min(256, mb)

    def block(b, _):
        k, i = b // ni, b % ni
        slot = lax.rem(b, SLOTS)
        gram_copy(b).wait()
        w = ft[pl.ds(pl.multiple_of(k * kb, kb), kb), :]

        def inner(m, _):
            rows_at = pl.multiple_of(m * step, step)
            acc = jnp.dot(gram[slot, pl.ds(rows_at, step), :].astype(BF16), w, preferred_element_type=F32)
            at = pl.ds(pl.multiple_of(i * mb + m * step, step), step)

            @pl.when(k == 0)
            def _():
                pt[at, :] = acc

            @pl.when(k > 0)
            def _():
                pt[at, :] = pt[at, :] + acc
            return 0

        lax.fori_loop(0, mb // step, inner, 0)

        @pl.when(b + SLOTS < blocks)
        def _():
            gram_copy(b + SLOTS).start()
        return 0

    lax.fori_loop(0, blocks, block, 0)

    tile = 128
    for j in range(grows // tile):
        t = pt[j * tile:(j + 1) * tile, :].T
        per = pre.shape[2] // tile
        pre[j // per, :, (j % per) * tile:(j % per + 1) * tile] = t[:nq] + t[nq:2 * nq]
    other = lax.rem(s + 1, subs)
    x_sub = remote(pre.at[other], sub_in, ps_sem.at[0], ps_sem.at[1], r, c, other)
    x_sub.start()
    x_sub.wait()
    pre[s] = pre[s] + sub_in[...]
    x_cols = [remote(pre.at[s], col_in.at[c], pc_send.at[d], pc_recv.at[d], r, lax.rem(c + d, cols), s)
              for d in range(1, cols)]
    for x in x_cols:
        x.start()
    col_in[c] = pre[s]
    for x in x_cols:
        x.wait()
    total = col_in[0]
    for o in range(1, cols):
        total = total + col_in[o]
    loads[4].wait()
    score = lax.dot_general(jnp.concatenate(split(total), axis=0), store[...], (((1,), (1,)), ((), ())),
                            preferred_element_type=F32)
    score = score[:nq] + score[nq:]

    hq = nq // subs
    for o in range(subs):
        own[o] = score[o * hq:(o + 1) * hq]
    x_half = remote(own.at[other], half_in, ss_sem.at[0], ss_sem.at[1], r, c, other)
    x_half.start()
    x_half.wait()
    own_s[...] = own[s] + half_in[...]
    x_rows = [remote(own_s, half_all.at[r], sz_send.at[d], sz_recv.at[d], lax.rem(r + d, rows), c, s)
              for d in range(1, rows)]
    for x in x_rows:
        x.start()
    half_all[r] = own_s[...]
    for x in x_rows:
        x.wait()
    total = half_all[0]
    for o in range(1, rows):
        total = total + half_all[o]
    half_out[s] = total
    x_out = remote(half_out.at[s], half_out.at[s], sf_sem.at[0], sf_sem.at[1], r, c, other)
    x_out.start()
    x_out.wait()
    for o in range(subs):
        out[o * hq:(o + 1) * hq, :] = half_out[o]


def body(sizes, query_acts, query_grads, proj_in, proj_out, inverse_gram, store_slab):
    rows, cols, subs = sizes
    queries, tokens, depth = query_acts.shape
    kin, kout = proj_in.shape[1], proj_out.shape[1]
    planes = cols * subs
    nq = planes * queries
    aw = kin // planes
    grows, gcols = inverse_gram.shape
    mb, kb = min(512, grows), min(2048, gcols)
    examples, width = store_slab.shape
    half = queries // 2
    hq = nq // subs
    dma = pltpu.SemaphoreType.DMA
    lanes = -(-2 * nq // 128) * 128
    scratch = [
        pltpu.VMEM(query_acts.shape, BF16), pltpu.VMEM(query_grads.shape, BF16),
        pltpu.VMEM(proj_in.shape, BF16), pltpu.VMEM(proj_out.shape, BF16),
        pltpu.VMEM((SLOTS, mb, kb), F32), pltpu.VMEM(store_slab.shape, BF16),
        pltpu.VMEM((queries, 2, tokens, kin), F32), pltpu.VMEM((queries, 2, tokens, kin), F32),
        pltpu.VMEM((half, kin, kout), F32), pltpu.VMEM((planes, queries, aw, kout), F32),
        pltpu.VMEM((gcols, lanes), BF16), pltpu.VMEM((grows, lanes), F32),
        pltpu.VMEM((subs, nq, width), F32), pltpu.VMEM((nq, width), F32), pltpu.VMEM((cols, nq, width), F32),
        pltpu.VMEM((subs, hq, examples), F32), pltpu.VMEM((hq, examples), F32), pltpu.VMEM((hq, examples), F32),
        pltpu.VMEM((rows, hq, examples), F32), pltpu.VMEM((subs, hq, examples), F32),
        dma((5,)), dma((SLOTS,)), dma((queries, 2)), dma((queries, 2)),
        dma((half, planes)), dma((half, planes)), dma((half,)), dma((queries,)), dma((queries,)),
        dma((2,)), dma((cols,)), dma((cols,)), dma((2,)), dma((rows,)), dma((rows,)), dma((1,)), dma((2,)),
    ]
    return pl.pallas_call(
        functools.partial(kernel, rows, cols, subs),
        out_shape=jax.ShapeDtypeStruct((nq, examples), F32),
        in_specs=[pl.BlockSpec(memory_space=pltpu.HBM)] * 6,
        out_specs=pl.BlockSpec(memory_space=pltpu.VMEM),
        scratch_shapes=scratch,
        compiler_params=pltpu.CompilerParams(
            collective_id=0, has_side_effects=True, vmem_limit_bytes=67043328),
        name="influence",
    )(query_acts, query_grads, proj_in, proj_out, inverse_gram, store_slab)


def solution(mesh):
    sizes = (mesh.shape["row"], mesh.shape["col"], mesh.shape["sub"])
    return jax.shard_map(
        functools.partial(body, sizes),
        mesh=mesh,
        in_specs=(
            P(("groups", "col", "sub"), None, "row"),
            P(("groups", "col", "sub"), None, "row"),
            P("row", None),
            P("row", None),
            P("row", ("col", "sub")),
            P(("groups", "col"), ("row", "sub")),
        ),
        out_specs=P("groups", "col"),
        check_vma=False,
    )
```

```python
import functools

import jax
import jax.numpy as jnp
from jax import lax
from jax.experimental import pallas as pl
from jax.experimental.pallas import tpu as pltpu
from jax.sharding import PartitionSpec as P

F32, BF16 = jnp.float32, jnp.bfloat16
SLOTS = 11
LAG = 2


def split(x):
    hi = x.astype(BF16)
    return hi, (x - hi.astype(F32)).astype(BF16)


def kernel(rows, cols, subs, acts_h, grads_h, pin_h, pout_h, gram_h, store_h, out,
           acts, grads, pin, pout, gram, store, part, recv, feats, fbuf, ft, pre, sub_in, col_in,
           own, own_s, half_in, half_all, half_out,
           in_sem, gram_sem, rs_send, rs_recv, fx_send, fx_recv, fx_local, fz_send, fz_recv,
           ps_send, ps_recv, pc_send, pc_recv, ss_sem, sz_send, sz_recv, sl_sem, sf_sem):
    g, r, c, s = (lax.axis_index(n) for n in ("groups", "row", "col", "sub"))
    queries = acts.shape[0]
    half = queries // 2
    planes = cols * subs
    me = c * subs + s
    aw = fbuf.shape[2]
    mb, kb = gram.shape[1], gram.shape[2]
    grows, gcols = gram_h.shape
    nk, ni = gcols // kb, grows // mb
    blocks = nk * ni
    per = ni // subs
    other = lax.rem(s + 1, subs)

    def dev(row, col, sub):
        return {"groups": g, "row": row, "col": col, "sub": sub}

    def remote(src, dst, send, rcv, row, col, sub):
        return pltpu.make_async_remote_copy(
            src_ref=src, dst_ref=dst, send_sem=send, recv_sem=rcv,
            device_id=dev(row, col, sub), device_id_type=pl.DeviceIdType.MESH)

    loads = [pltpu.make_async_copy(a, b, in_sem.at[i]) for i, (a, b) in enumerate(
        ((pin_h, pin), (pout_h, pout), (acts_h, acts), (grads_h, grads), (store_h, store)))]
    for l in loads[:4]:
        l.start()

    def gram_copy(b):
        n, k = b // nk, b % nk
        i = lax.rem(other * per + n, ni)
        slot = lax.rem(b, SLOTS)
        return pltpu.make_async_copy(
            gram_h.at[pl.ds(pl.multiple_of(i * mb, mb), mb), pl.ds(pl.multiple_of(k * kb, kb), kb)],
            gram.at[slot], gram_sem.at[slot])

    for b in range(min(SLOTS, blocks)):
        gram_copy(b).start()
    loads[4].start()

    barrier = pltpu.get_barrier_semaphore()
    count = 0
    for d in range(1, rows):
        pl.semaphore_signal(barrier, inc=1, device_id=dev(lax.rem(r + d, rows), c, s), device_id_type=pl.DeviceIdType.MESH)
        count += 1
    for d in range(1, planes):
        o = lax.rem(me + d, planes)
        pl.semaphore_signal(barrier, inc=1, device_id=dev(r, o // subs, lax.rem(o, subs)), device_id_type=pl.DeviceIdType.MESH)
        count += 1

    def project(q):
        part[q, 0] = jnp.dot(acts[q], pin[...], preferred_element_type=F32)
        part[q, 1] = jnp.dot(grads[q], pout[...], preferred_element_type=F32)

    for l in loads[:4]:
        l.wait()
    for q in range(queries):
        project(q)
    pl.semaphore_wait(barrier, count)

    starts = (r == 0, r == rows - 1)
    ends = (r == rows - 1, r == 0)
    ahead = (jnp.minimum(r + 1, rows - 1), jnp.maximum(r - 1, 0))
    behind = (jnp.maximum(r - 1, 0), jnp.minimum(r + 1, rows - 1))

    def rs_copy(h, q, w):
        return remote(part.at[q, w], recv.at[q, w], rs_send.at[q, w], rs_recv.at[q, w], ahead[h], c, s)

    def fx_copy(q, d):
        o = lax.rem(me + d, planes)
        return remote(feats.at[lax.rem(q, half), pl.ds(pl.multiple_of(o * aw, aw), aw)], fbuf.at[me, q],
                      fx_send.at[lax.rem(q, half), d], fx_recv.at[lax.rem(q, half), d], r, o // subs, lax.rem(o, subs))

    def fx_own(q):
        return pltpu.make_async_copy(feats.at[lax.rem(q, half), pl.ds(pl.multiple_of(me * aw, aw), aw)],
                                     fbuf.at[me, q], fx_local.at[lax.rem(q, half)])

    def fz_copy(h, q):
        return remote(fbuf.at[:, q], fbuf.at[:, q], fz_send.at[q], fz_recv.at[q], behind[h], c, s)

    def send_row(h, q):
        for d in range(1, planes):
            fx_copy(q, d).wait()
        fx_own(q).wait()
        fz_copy(h, q).start()

    def sums(t, _):
        for h in range(2):
            j = t - LAG * (r if h == 0 else rows - 1 - r)
            k, w = j // 2, lax.rem(j, 2)
            q = h * half + k
            live = jnp.logical_and(j >= 0, j < 2 * half)

            @pl.when(jnp.logical_and(live, jnp.logical_not(starts[h])))
            def _():
                rs_copy(h, q, w).wait_recv()
                part[q, w] = part[q, w] + recv[q, w]

            @pl.when(jnp.logical_and(live, jnp.logical_not(ends[h])))
            def _():
                rs_copy(h, q, w).start()

            @pl.when(jnp.logical_and(jnp.logical_and(live, ends[h]), w == 1))
            def _():
                feats[k] = jnp.dot(part[q, 0].T, part[q, 1], precision=lax.Precision.HIGHEST,
                                   preferred_element_type=F32)
                for d in range(1, planes):
                    fx_copy(q, d).start()
                fx_own(q).start()

                @pl.when(k > 0)
                def _():
                    send_row(h, q - 1)
        return 0

    lax.fori_loop(0, 2 * half + LAG * (rows - 1), sums, 0)
    for h in range(2):
        @pl.when(ends[h])
        def _():
            send_row(h, h * half + half - 1)

    def back(t, _):
        for h in range(2):
            k = t - LAG * (rows - 1 - r if h == 0 else r)
            q = h * half + k
            live = jnp.logical_and(k >= 0, k < half)

            @pl.when(jnp.logical_and(live, jnp.logical_not(ends[h])))
            def _():
                fz_copy(h, q).wait_recv()

            @pl.when(jnp.logical_and(live, jnp.logical_not(jnp.logical_or(starts[h], ends[h]))))
            def _():
                fz_copy(h, q).start()
        return 0

    lax.fori_loop(0, half + LAG * (rows - 1), back, 0)
    for k in range(half):
        for h in range(2):
            q = h * half + k

            @pl.when(jnp.logical_not(starts[h]))
            def _():
                fz_copy(h, q).wait_send()

            @pl.when(jnp.logical_not(ends[h]))
            def _():
                for w in range(2):
                    rs_copy(h, q, w).wait_send()

    nq = planes * queries
    width = ft.shape[1]
    for a in range(aw):
        x = fbuf[:, :, a, :].reshape(nq, fbuf.shape[3])
        hi, lo = split(x)
        hi, lo = hi.astype(F32), lo.astype(F32)
        rest = [jnp.zeros((width - 2 * nq, x.shape[1]), F32)] if width > 2 * nq else []
        y = jnp.concatenate([hi, lo] + rest, axis=0)
        ft[a * x.shape[1]:(a + 1) * x.shape[1], :] = y.T.astype(BF16)

    step = min(256, mb)

    def sub_copy(p):
        return remote(pre.at[p], sub_in.at[p], ps_send.at[p], ps_recv.at[p], r, c, other)

    def col_copy(p, d):
        return remote(pre.at[per + p], col_in.at[c, p], pc_send.at[d, p], pc_recv.at[d, p], r, lax.rem(c + d, cols), s)

    def block(n, _):
        for k in range(nk):
            gram_copy(n * nk + k).wait()
        for m in range(mb // step):
            acc = None
            for k in range(nk):
                slot = lax.rem(n * nk + k, SLOTS)
                term = jnp.dot(gram[slot, m * step:(m + 1) * step, :].astype(BF16), ft[k * kb:(k + 1) * kb, :],
                               preferred_element_type=F32)
                acc = term if acc is None else acc + term
            t = acc.T
            pre[n, :, m * step:(m + 1) * step] = t[:nq] + t[nq:2 * nq]
        for k in range(nk):
            @pl.when(n * nk + k + SLOTS < blocks)
            def _():
                gram_copy(n * nk + k + SLOTS).start()

        @pl.when(n < per)
        def _():
            sub_copy(n).start()

        @pl.when(n >= per)
        def _():
            sub_copy(n - per).wait_recv()
            pre[n] = pre[n] + sub_in[n - per]
            for d in range(1, cols):
                col_copy(n - per, d).start()
            col_in[c, n - per] = pre[n]
        return 0

    lax.fori_loop(0, ni, block, 0)
    loads[4].wait()
    score = None
    for p in range(per):
        for d in range(1, cols):
            col_copy(p, d).wait()
        sub_copy(p).wait_send()
        total = col_in[0, p]
        for o in range(1, cols):
            total = total + col_in[o, p]
        term = lax.dot_general(jnp.concatenate(split(total), axis=0), store[:, p * mb:(p + 1) * mb],
                               (((1,), (1,)), ((), ())), preferred_element_type=F32)
        score = term if score is None else score + term
    score = score[:nq] + score[nq:]

    hq = nq // subs
    for o in range(subs):
        own[o] = score[o * hq:(o + 1) * hq]
    x_half = remote(own.at[other], half_in, ss_sem.at[0], ss_sem.at[1], r, c, other)
    x_half.start()
    x_half.wait()
    own_s[...] = own[s] + half_in[...]
    x_rows = [remote(own_s, half_all.at[r], sz_send.at[d], sz_recv.at[d], lax.rem(r + d, rows), c, s)
              for d in range(1, rows)]
    for x in x_rows:
        x.start()
    half_all[r] = own_s[...]
    for x in x_rows:
        x.wait()
    total = half_all[0]
    for o in range(1, rows):
        total = total + half_all[o]
    half_out[s] = total
    x_out = remote(half_out.at[s], half_out.at[s], sf_sem.at[0], sf_sem.at[1], r, c, other)
    x_out.start()
    x_out.wait()
    for o in range(subs):
        out[o * hq:(o + 1) * hq, :] = half_out[o]


def body(sizes, query_acts, query_grads, proj_in, proj_out, inverse_gram, store_slab):
    rows, cols, subs = sizes
    queries, tokens, depth = query_acts.shape
    kin, kout = proj_in.shape[1], proj_out.shape[1]
    planes = cols * subs
    nq = planes * queries
    aw = kin // planes
    grows, gcols = inverse_gram.shape
    mb, kb = min(512, grows // subs), min(2048, gcols)
    per = grows // subs // mb
    examples, width = store_slab.shape
    half = queries // 2
    hq = nq // subs
    dma = pltpu.SemaphoreType.DMA
    lanes = -(-2 * nq // 128) * 128
    scratch = [
        pltpu.VMEM(query_acts.shape, BF16), pltpu.VMEM(query_grads.shape, BF16),
        pltpu.VMEM(proj_in.shape, BF16), pltpu.VMEM(proj_out.shape, BF16),
        pltpu.VMEM((SLOTS, mb, kb), F32), pltpu.VMEM(store_slab.shape, BF16),
        pltpu.VMEM((queries, 2, tokens, kin), F32), pltpu.VMEM((queries, 2, tokens, kin), F32),
        pltpu.VMEM((half, kin, kout), F32), pltpu.VMEM((planes, queries, aw, kout), F32),
        pltpu.VMEM((gcols, lanes), BF16),
        pltpu.VMEM((subs * per, nq, mb), F32), pltpu.VMEM((per, nq, mb), F32),
        pltpu.VMEM((cols, per, nq, mb), F32),
        pltpu.VMEM((subs, hq, examples), F32), pltpu.VMEM((hq, examples), F32), pltpu.VMEM((hq, examples), F32),
        pltpu.VMEM((rows, hq, examples), F32), pltpu.VMEM((subs, hq, examples), F32),
        dma((5,)), dma((SLOTS,)), dma((queries, 2)), dma((queries, 2)),
        dma((half, planes)), dma((half, planes)), dma((half,)), dma((queries,)), dma((queries,)),
        dma((per,)), dma((per,)), dma((cols, per)), dma((cols, per)), dma((2,)), dma((rows,)), dma((rows,)), dma((1,)), dma((2,)),
    ]
    return pl.pallas_call(
        functools.partial(kernel, rows, cols, subs),
        out_shape=jax.ShapeDtypeStruct((nq, examples), F32),
        in_specs=[pl.BlockSpec(memory_space=pltpu.HBM)] * 6,
        out_specs=pl.BlockSpec(memory_space=pltpu.VMEM),
        scratch_shapes=scratch,
        compiler_params=pltpu.CompilerParams(
            collective_id=0, has_side_effects=True, vmem_limit_bytes=67043328),
        name="influence",
    )(query_acts, query_grads, proj_in, proj_out, inverse_gram, store_slab)


def solution(mesh):
    sizes = (mesh.shape["row"], mesh.shape["col"], mesh.shape["sub"])
    return jax.shard_map(
        functools.partial(body, sizes),
        mesh=mesh,
        in_specs=(
            P(("groups", "col", "sub"), None, "row"),
            P(("groups", "col", "sub"), None, "row"),
            P("row", None),
            P("row", None),
            P("row", ("col", "sub")),
            P(("groups", "col"), ("row", "sub")),
        ),
        out_specs=P("groups", "col"),
        check_vma=False,
    )
```

```python
import functools

import jax
import jax.numpy as jnp
from jax import lax
from jax.experimental import pallas as pl
from jax.experimental.pallas import tpu as pltpu
from jax.sharding import PartitionSpec as P

F32, BF16 = jnp.float32, jnp.bfloat16
SLOTS = 11
LAG = 2


def split(x):
    hi = x.astype(BF16)
    return hi, (x - hi.astype(F32)).astype(BF16)


def kernel(rows, cols, subs, acts_h, grads_h, pin_h, pout_h, gram_h, store_h, out,
           acts, grads, pin, pout, gram, store, part, recv, feats, fbuf, ft, pre, sub_in, col_in,
           own, own_s, half_in, half_all, half_out,
           in_sem, gram_sem, rs_send, rs_recv, fx_send, fx_recv, fx_local, fz_send, fz_recv,
           ps_send, ps_recv, pc_send, pc_recv, ss_sem, sz_send, sz_recv, sl_sem, sf_sem):
    g, r, c, s = (lax.axis_index(n) for n in ("groups", "row", "col", "sub"))
    queries = acts.shape[0]
    half = queries // 2
    planes = cols * subs
    me = c * subs + s
    aw = fbuf.shape[2]
    mb, kb = gram.shape[1], gram.shape[2]
    grows, gcols = gram_h.shape
    nk, ni = gcols // kb, grows // mb
    blocks = nk * ni
    per = ni // subs
    other = lax.rem(s + 1, subs)

    def dev(row, col, sub):
        return {"groups": g, "row": row, "col": col, "sub": sub}

    def remote(src, dst, send, rcv, row, col, sub):
        return pltpu.make_async_remote_copy(
            src_ref=src, dst_ref=dst, send_sem=send, recv_sem=rcv,
            device_id=dev(row, col, sub), device_id_type=pl.DeviceIdType.MESH)

    loads = [pltpu.make_async_copy(a, b, in_sem.at[i]) for i, (a, b) in enumerate(
        ((pin_h, pin), (pout_h, pout), (acts_h, acts), (grads_h, grads), (store_h, store)))]
    for l in loads[:4]:
        l.start()

    def gram_copy(b):
        n, k = b // nk, b % nk
        i = lax.rem(other * per + n, ni)
        slot = lax.rem(b, SLOTS)
        return pltpu.make_async_copy(
            gram_h.at[pl.ds(pl.multiple_of(i * mb, mb), mb), pl.ds(pl.multiple_of(k * kb, kb), kb)],
            gram.at[slot], gram_sem.at[slot])

    barrier = pltpu.get_barrier_semaphore()
    count = 0
    for d in range(1, rows):
        pl.semaphore_signal(barrier, inc=1, device_id=dev(lax.rem(r + d, rows), c, s), device_id_type=pl.DeviceIdType.MESH)
        count += 1
    for d in range(1, planes):
        o = lax.rem(me + d, planes)
        pl.semaphore_signal(barrier, inc=1, device_id=dev(r, o // subs, lax.rem(o, subs)), device_id_type=pl.DeviceIdType.MESH)
        count += 1

    def project(q):
        part[q, 0] = jnp.dot(acts[q], pin[...], preferred_element_type=F32)
        part[q, 1] = jnp.dot(grads[q], pout[...], preferred_element_type=F32)

    for l in loads[:4]:
        l.wait()
    for b in range(min(SLOTS, blocks)):
        gram_copy(b).start()
    loads[4].start()
    for q in range(queries):
        project(q)
    pl.semaphore_wait(barrier, count)

    starts = (r == 0, r == rows - 1)
    ends = (r == rows - 1, r == 0)
    ahead = (jnp.minimum(r + 1, rows - 1), jnp.maximum(r - 1, 0))
    behind = (jnp.maximum(r - 1, 0), jnp.minimum(r + 1, rows - 1))

    def rs_copy(h, q, w):
        return remote(part.at[q, w], recv.at[q, w], rs_send.at[q, w], rs_recv.at[q, w], ahead[h], c, s)

    def fx_copy(q, d):
        o = lax.rem(me + d, planes)
        return remote(feats.at[lax.rem(q, half), pl.ds(pl.multiple_of(o * aw, aw), aw)], fbuf.at[me, q],
                      fx_send.at[lax.rem(q, half), d], fx_recv.at[lax.rem(q, half), d], r, o // subs, lax.rem(o, subs))

    def fx_own(q):
        return pltpu.make_async_copy(feats.at[lax.rem(q, half), pl.ds(pl.multiple_of(me * aw, aw), aw)],
                                     fbuf.at[me, q], fx_local.at[lax.rem(q, half)])

    def fz_copy(h, q):
        return remote(fbuf.at[:, q], fbuf.at[:, q], fz_send.at[q], fz_recv.at[q], behind[h], c, s)

    def send_row(h, q):
        for d in range(1, planes):
            fx_copy(q, d).wait()
        fx_own(q).wait()
        fz_copy(h, q).start()

    def sums(t, _):
        for h in range(2):
            j = t - LAG * (r if h == 0 else rows - 1 - r)
            k, w = j // 2, lax.rem(j, 2)
            q = h * half + k
            live = jnp.logical_and(j >= 0, j < 2 * half)

            @pl.when(jnp.logical_and(live, jnp.logical_not(starts[h])))
            def _():
                rs_copy(h, q, w).wait_recv()
                part[q, w] = part[q, w] + recv[q, w]

            @pl.when(jnp.logical_and(live, jnp.logical_not(ends[h])))
            def _():
                rs_copy(h, q, w).start()

            @pl.when(jnp.logical_and(jnp.logical_and(live, ends[h]), w == 1))
            def _():
                feats[k] = jnp.dot(part[q, 0].T, part[q, 1], precision=lax.Precision.HIGHEST,
                                   preferred_element_type=F32)
                for d in range(1, planes):
                    fx_copy(q, d).start()
                fx_own(q).start()

                @pl.when(k > 0)
                def _():
                    send_row(h, q - 1)
        return 0

    lax.fori_loop(0, 2 * half + LAG * (rows - 1), sums, 0)
    for h in range(2):
        @pl.when(ends[h])
        def _():
            send_row(h, h * half + half - 1)

    def back(t, _):
        for h in range(2):
            k = t - LAG * (rows - 1 - r if h == 0 else r)
            q = h * half + k
            live = jnp.logical_and(k >= 0, k < half)

            @pl.when(jnp.logical_and(live, jnp.logical_not(ends[h])))
            def _():
                fz_copy(h, q).wait_recv()

            @pl.when(jnp.logical_and(live, jnp.logical_not(jnp.logical_or(starts[h], ends[h]))))
            def _():
                fz_copy(h, q).start()
        return 0

    lax.fori_loop(0, half + LAG * (rows - 1), back, 0)
    for k in range(half):
        for h in range(2):
            q = h * half + k

            @pl.when(jnp.logical_not(starts[h]))
            def _():
                fz_copy(h, q).wait_send()

            @pl.when(jnp.logical_not(ends[h]))
            def _():
                for w in range(2):
                    rs_copy(h, q, w).wait_send()

    nq = planes * queries
    width = ft.shape[1]
    for a in range(aw):
        x = fbuf[:, :, a, :].reshape(nq, fbuf.shape[3])
        hi, lo = split(x)
        hi, lo = hi.astype(F32), lo.astype(F32)
        rest = [jnp.zeros((width - 2 * nq, x.shape[1]), F32)] if width > 2 * nq else []
        y = jnp.concatenate([hi, lo] + rest, axis=0)
        ft[a * x.shape[1]:(a + 1) * x.shape[1], :] = y.T.astype(BF16)

    step = min(256, mb)

    def sub_copy(p):
        return remote(pre.at[p], sub_in.at[p], ps_send.at[p], ps_recv.at[p], r, c, other)

    def col_copy(p, d):
        return remote(pre.at[per + p], col_in.at[c, p], pc_send.at[d, p], pc_recv.at[d, p], r, lax.rem(c + d, cols), s)

    def block(n, _):
        for k in range(nk):
            gram_copy(n * nk + k).wait()
        for m in range(mb // step):
            acc = None
            for k in range(nk):
                slot = lax.rem(n * nk + k, SLOTS)
                term = jnp.dot(gram[slot, m * step:(m + 1) * step, :].astype(BF16), ft[k * kb:(k + 1) * kb, :],
                               preferred_element_type=F32)
                acc = term if acc is None else acc + term
            t = acc.T
            pre[n, :, m * step:(m + 1) * step] = t[:nq] + t[nq:2 * nq]
        for k in range(nk):
            @pl.when(n * nk + k + SLOTS < blocks)
            def _():
                gram_copy(n * nk + k + SLOTS).start()

        @pl.when(n < per)
        def _():
            sub_copy(n).start()

        @pl.when(n >= per)
        def _():
            sub_copy(n - per).wait_recv()
            pre[n] = pre[n] + sub_in[n - per]
            for d in range(1, cols):
                col_copy(n - per, d).start()
            col_in[c, n - per] = pre[n]
        return 0

    lax.fori_loop(0, ni, block, 0)
    loads[4].wait()
    score = None
    for p in range(per):
        for d in range(1, cols):
            col_copy(p, d).wait()
        sub_copy(p).wait_send()
        total = col_in[0, p]
        for o in range(1, cols):
            total = total + col_in[o, p]
        term = lax.dot_general(jnp.concatenate(split(total), axis=0), store[:, p * mb:(p + 1) * mb],
                               (((1,), (1,)), ((), ())), preferred_element_type=F32)
        score = term if score is None else score + term
    score = score[:nq] + score[nq:]

    hq = nq // subs
    for o in range(subs):
        own[o] = score[o * hq:(o + 1) * hq]
    x_half = remote(own.at[other], half_in, ss_sem.at[0], ss_sem.at[1], r, c, other)
    x_half.start()
    x_half.wait()
    own_s[...] = own[s] + half_in[...]
    x_rows = [remote(own_s, half_all.at[r], sz_send.at[d], sz_recv.at[d], lax.rem(r + d, rows), c, s)
              for d in range(1, rows)]
    for x in x_rows:
        x.start()
    half_all[r] = own_s[...]
    for x in x_rows:
        x.wait()
    total = half_all[0]
    for o in range(1, rows):
        total = total + half_all[o]
    half_out[s] = total
    x_out = remote(half_out.at[s], half_out.at[s], sf_sem.at[0], sf_sem.at[1], r, c, other)
    x_out.start()
    x_out.wait()
    for o in range(subs):
        out[o * hq:(o + 1) * hq, :] = half_out[o]


def body(sizes, query_acts, query_grads, proj_in, proj_out, inverse_gram, store_slab):
    rows, cols, subs = sizes
    queries, tokens, depth = query_acts.shape
    kin, kout = proj_in.shape[1], proj_out.shape[1]
    planes = cols * subs
    nq = planes * queries
    aw = kin // planes
    grows, gcols = inverse_gram.shape
    mb, kb = min(512, grows // subs), min(2048, gcols)
    per = grows // subs // mb
    examples, width = store_slab.shape
    half = queries // 2
    hq = nq // subs
    dma = pltpu.SemaphoreType.DMA
    lanes = -(-2 * nq // 128) * 128
    scratch = [
        pltpu.VMEM(query_acts.shape, BF16), pltpu.VMEM(query_grads.shape, BF16),
        pltpu.VMEM(proj_in.shape, BF16), pltpu.VMEM(proj_out.shape, BF16),
        pltpu.VMEM((SLOTS, mb, kb), F32), pltpu.VMEM(store_slab.shape, BF16),
        pltpu.VMEM((queries, 2, tokens, kin), F32), pltpu.VMEM((queries, 2, tokens, kin), F32),
        pltpu.VMEM((half, kin, kout), F32), pltpu.VMEM((planes, queries, aw, kout), F32),
        pltpu.VMEM((gcols, lanes), BF16),
        pltpu.VMEM((subs * per, nq, mb), F32), pltpu.VMEM((per, nq, mb), F32),
        pltpu.VMEM((cols, per, nq, mb), F32),
        pltpu.VMEM((subs, hq, examples), F32), pltpu.VMEM((hq, examples), F32), pltpu.VMEM((hq, examples), F32),
        pltpu.VMEM((rows, hq, examples), F32), pltpu.VMEM((subs, hq, examples), F32),
        dma((5,)), dma((SLOTS,)), dma((queries, 2)), dma((queries, 2)),
        dma((half, planes)), dma((half, planes)), dma((half,)), dma((queries,)), dma((queries,)),
        dma((per,)), dma((per,)), dma((cols, per)), dma((cols, per)), dma((2,)), dma((rows,)), dma((rows,)), dma((1,)), dma((2,)),
    ]
    return pl.pallas_call(
        functools.partial(kernel, rows, cols, subs),
        out_shape=jax.ShapeDtypeStruct((nq, examples), F32),
        in_specs=[pl.BlockSpec(memory_space=pltpu.HBM)] * 6,
        out_specs=pl.BlockSpec(memory_space=pltpu.VMEM),
        scratch_shapes=scratch,
        compiler_params=pltpu.CompilerParams(
            collective_id=0, has_side_effects=True, vmem_limit_bytes=67043328),
        name="influence",
    )(query_acts, query_grads, proj_in, proj_out, inverse_gram, store_slab)


def solution(mesh):
    sizes = (mesh.shape["row"], mesh.shape["col"], mesh.shape["sub"])
    return jax.shard_map(
        functools.partial(body, sizes),
        mesh=mesh,
        in_specs=(
            P(("groups", "col", "sub"), None, "row"),
            P(("groups", "col", "sub"), None, "row"),
            P("row", None),
            P("row", None),
            P("row", ("col", "sub")),
            P(("groups", "col"), ("row", "sub")),
        ),
        out_specs=P("groups", "col"),
        check_vma=False,
    )
```
